32 devices in a mesh: dp: 8 (over z, y), fsdp: 4 (over x, core).
Axes of the slice: x: 2, y: 2, z: 4, core: 2. Of those that a mesh axis runs over, the one named last changes fastest.
Arguments:
- inputs: float32 [32, 512, 1536], P(('dp', 'fsdp')), may hold values from -6 to 6
- segments: int32 [32, 512], P(('dp', 'fsdp')), may hold values from 0 to 2, as said below
- cotangent: float32 [32, 512, 1536], P(('dp', 'fsdp')), may hold values from -6 to 6
- params: float32 [1, 14647296], P(None, ('dp', 'fsdp')), as said below
- moment_one: float32 [1, 14647296], P(None, ('dp', 'fsdp')), may hold values from -180 to 180
- moment_two: float32 [1, 14647296], P(None, ('dp', 'fsdp')), may hold values from 100 to 10000
Outputs:
- output: float32 [32, 512, 1536], P(('dp', 'fsdp'))
- grad_inputs: float32 [32, 512, 1536], P(('dp', 'fsdp'))
- grads: float32 [1, 14647296], P(None, ('dp', 'fsdp'))
- new_params: float32 [1, 14647296], P(None, ('dp', 'fsdp'))
- new_moment_one: float32 [1, 14647296], P(None, ('dp', 'fsdp'))
- new_moment_two: float32 [1, 14647296], P(None, ('dp', 'fsdp'))
The draws below stay inside these ranges and needn't reach their ends.
Inputs may be any that keep to these rules, and one draw needn't show every extreme that they name: `segments`: within each sequence the numbers never fall, are 0 at the first position and 2 at the last; a document is a run of positions with one number. `params`: holds each layer's pieces in the layout of the steps.
All inputs are finite; a program needn't handle non-finite values.
Results may differ from the reference program's by a relative error of at most 0.014.
Values may be sent and summed in bfloat16 or wider, within the bound.
No kernel may reach another device: no remote copies, remote signals or barrier semaphores. Data moves between devices by JAX's collectives and lax.ppermute only.
A program may use at most 384 MiB of HBM per device.

```python
import math
import jax
import jax.numpy as jnp
from jax import lax

D = 1536
DI = 3072
HEADS = 48
STATE = 128
HEADDIM = 64
KCONV = 4
SEQLEN = 512
LAYERS = 1
STEP = 4
SEQ_DEV = 1
DCONV = 3328
DPROJ = 6448
PFLAT = 14647296
SEQS = 32


def draw_segments(key, part):
    cut_points = jax.random.randint(key, (SEQS, 2), 1, SEQLEN)
    positions = jnp.arange(SEQLEN, dtype=jnp.int32)[None, :]
    first = (positions >= cut_points[:, 0:1]).astype(jnp.int32)
    second = (positions >= cut_points[:, 1:2]).astype(jnp.int32)
    return first + second


def draw_params(key, part):
    shape_all = (LAYERS, PFLAT)
    position = jnp.arange(PFLAT, dtype=jnp.int32)[None, :]
    normals = jax.random.normal(jax.random.fold_in(key, 11), shape_all, jnp.float32)
    evens = jax.random.uniform(jax.random.fold_in(key, 12), shape_all, jnp.float32)
    log_step = math.log(0.001) + evens * (math.log(0.1) - math.log(0.001))
    step_init = jnp.exp(log_step)
    dt_init = step_init + jnp.log(-jnp.expm1(-step_init))
    candidates = [normals * D ** (-0.5), normals * 0.4, normals * 0.3, dt_init, jnp.log(1.0 + 15.0 * evens), 0.5 + evens, 0.7 + 0.6 * evens, 0.7 + 0.6 * evens, normals * DI ** (-0.5)]
    lengths = [D * DPROJ, KCONV * DCONV, DCONV, HEADS, HEADS, HEADS, D, DI, DI * D]
    values = normals * 0.02
    start_at = 0
    for number, candidate in zip(lengths, candidates):
        inside = (position >= start_at) & (position < start_at + number)
        values = jnp.where(inside, candidate, values)
        start_at = start_at + number
    return values


def block_levels(own_key, extent, split, low, high):
    def one(dim, blocks):
        heights = jax.random.uniform(jax.random.fold_in(jax.random.fold_in(own_key, 6), dim), (blocks,), jnp.float32, low / len(split), high / len(split))
        return jnp.repeat(jnp.exp(heights), extent[dim] // blocks).reshape((-1,) + (1,) * (len(extent) - dim - 1))

    level = one(*split[0])
    for cut in split[1:]:
        level = level * one(*cut)
    return level


def scatter_about(rng, shape, deviation, reach, cuts=(), held_as=jnp.bfloat16):
    drawn = jax.random.normal(rng, shape, jnp.float32) * deviation
    if len(cuts) > 0:
        drawn = block_levels(rng, shape, cuts, -0.22, 0.18) * drawn
    return jnp.clip(drawn, min=-reach, max=reach).astype(held_as)


def setup_inputs(seed: int = 0) -> dict:
    arg_keys = jax.random.split(jax.random.key(seed), 7)
    inputs = scatter_about(arg_keys[0], (SEQS, SEQLEN, D), 1.0, 6.0, ((0, 32),), jnp.float32)
    segments = draw_segments(jax.random.fold_in(arg_keys[6], 71), 0)
    cotangent = scatter_about(arg_keys[2], (SEQS, SEQLEN, D), 1.0, 6.0, ((0, 32),), jnp.float32)
    params = draw_params(jax.random.fold_in(arg_keys[6], 71), 0)
    moment_one = scatter_about(arg_keys[4], (LAYERS, PFLAT), 30.0, 180.0, ((1, 32),), jnp.float32)
    moment_two = jnp.clip(jnp.exp(math.log(10000.0) - 4.6051702 * jax.random.uniform(arg_keys[5], (LAYERS, PFLAT), jnp.float32) ** block_levels(arg_keys[5], (LAYERS, PFLAT), ((1, 32),), -0.2, 0.2)), 100.0, 10000.0)
    return dict(inputs=inputs, segments=segments, cotangent=cotangent, params=params, moment_one=moment_one, moment_two=moment_two)


NORM_EPS = 1e-05
ADAM_EPS = 1e-08
LEARN_RATE = 0.003
DECAY_ONE = 0.9
DECAY_TWO = 0.95
WEIGHT_DECAY = 0.1

def piece_shapes():
    return [(D, DPROJ), (KCONV, DCONV), (DCONV,), (HEADS,), (HEADS,), (HEADS,), (D,), (DI,), (DI, D)]

def unpack(flat_vec):
    pieces = []
    offset = 0
    for shape_now in piece_shapes():
        number = math.prod(shape_now)
        pieces.append(flat_vec[offset:offset + number].reshape(shape_now))
        offset = offset + number
    return tuple(pieces)

def pack(pieces, length_all):
    joined = jnp.concatenate([member.reshape(-1) for member in pieces])
    return jnp.concatenate([joined, jnp.zeros((length_all - joined.shape[0],), jnp.float32)])

def shifted(values, shift_by):
    if shift_by == 0:
        return values
    filler = jnp.zeros((shift_by,) + values.shape[1:], values.dtype)
    return jnp.concatenate([filler, values[:-shift_by]], axis=0)

def pulled(values, shift_by):
    if shift_by == 0:
        return values
    filler = jnp.zeros((shift_by,) + values.shape[1:], values.dtype)
    return jnp.concatenate([values[shift_by:], filler], axis=0)

def same_doc(segment, shift_by):
    positions = jnp.arange(segment.shape[0], dtype=jnp.int32)
    usable = (positions >= shift_by) & (shifted(segment, shift_by) == segment)
    return usable.astype(jnp.float32)[:, None]

def silu_grad(values):
    sigmoid_v = jax.nn.sigmoid(values)
    return sigmoid_v * (1.0 + values * (1.0 - sigmoid_v))

def split_heads(values, per_head):
    seq_len = values.shape[0]
    return values.reshape(seq_len, HEADS // 4, 4, per_head).transpose(1, 0, 2, 3)

def join_heads(values):
    groups, seq_len, heads_in, per_head = values.shape
    return values.transpose(1, 0, 2, 3).reshape(seq_len, groups * heads_in * per_head)

def decay_table(cum_group, allowed):
    cum_t = cum_group.T
    differ = cum_t[:, :, None] - cum_t[:, None, :]
    return jnp.where(allowed[None], jnp.exp(jnp.where(allowed[None], differ, 0.0)), 0.0)

def input_norm(hidden, gain_one):
    inv_rms = lax.rsqrt(lax.optimization_barrier(jnp.mean(hidden * hidden, axis=-1, keepdims=True)) + NORM_EPS)
    normed = (hidden * inv_rms * gain_one.astype(jnp.float32)).astype(jnp.bfloat16)
    return (inv_rms, normed)

def ssd_forward(x_rows, step_size, cumul, gram, allowed, d_skip):
    x_groups = split_heads(x_rows, HEADDIM)
    cum_groups = split_heads(cumul, 1)[..., 0]
    step_groups = split_heads(step_size, 1)[..., 0]
    skip_groups = d_skip.astype(jnp.float32).reshape(HEADS // 4, 4)

    def one_group(group_in):
        x_group, cum_group, step_group, skip_group = group_in
        decays = decay_table(cum_group, allowed)
        mixing = (gram[None] * decays * step_group.T[:, None, :]).astype(jnp.bfloat16)
        x_float = x_group.astype(jnp.float32)
        result = jnp.einsum('hts,shp->thp', mixing.astype(jnp.float32), x_float)
        return result + skip_group[None, :, None] * x_float
    return join_heads(lax.map(one_group, (x_groups, cum_groups, step_groups, skip_groups)))

def mixer_state(projected, segment, weights):
    w_in, conv_w, conv_b, dt_bias, a_log, d_skip, gain_one, gain_two, w_out = weights
    seq_len = projected.shape[0]
    gate_in = projected[:, :DI]
    conv_in = projected[:, DI:DI + DCONV]
    dt_pre = projected[:, DI + DCONV:] + dt_bias.astype(jnp.float32)
    conv_out = conv_b.astype(jnp.float32) + jnp.zeros_like(conv_in)
    for shift_by in range(KCONV):
        conv_out = conv_out + conv_w[shift_by].astype(jnp.float32) * shifted(conv_in, shift_by) * same_doc(segment, shift_by)
    conv_act = jax.nn.silu(conv_out)
    x_rows = conv_act[:, :DI].astype(jnp.bfloat16)
    b_rows = conv_act[:, DI:DI + STATE].astype(jnp.bfloat16)
    c_rows = conv_act[:, DI + STATE:].astype(jnp.bfloat16)
    step_size = jax.nn.softplus(dt_pre)
    rate_vec = -jnp.exp(a_log.astype(jnp.float32))
    cumul = jnp.cumsum(step_size * rate_vec[None, :], axis=0)
    gram = jnp.dot(c_rows, b_rows.T, preferred_element_type=jnp.float32)
    positions = jnp.arange(seq_len, dtype=jnp.int32)
    allowed = (positions[:, None] >= positions[None, :]) & (segment[:, None] == segment[None, :])
    ssd_out = ssd_forward(x_rows, step_size, cumul, gram, allowed, d_skip)
    gate_act = jax.nn.silu(gate_in)
    gated_out = ssd_out * gate_act
    inv_rms_two = lax.rsqrt(lax.optimization_barrier(jnp.mean(gated_out * gated_out, axis=-1, keepdims=True)) + NORM_EPS)
    normed_out = (gated_out * inv_rms_two * gain_two.astype(jnp.float32)).astype(jnp.bfloat16)
    return dict(gate_in=gate_in, conv_in=conv_in, dt_pre=dt_pre, conv_out=conv_out, x_rows=x_rows, b_rows=b_rows, c_rows=c_rows, step_size=step_size, rate_vec=rate_vec, cumul=cumul, gram=gram, allowed=allowed, ssd_out=ssd_out, gate_act=gate_act, gated_out=gated_out, inv_rms_two=inv_rms_two, normed_out=normed_out)

def layer_forward(hidden, segment, weights):
    inv_rms, normed = input_norm(hidden, weights[6])
    projected = jnp.dot(normed, weights[0], preferred_element_type=jnp.float32)
    parts_now = mixer_state(projected, segment, weights)
    branch = jnp.dot(parts_now['normed_out'], weights[8], preferred_element_type=jnp.float32)
    return (projected, hidden + branch)

def ssd_backward(d_ssd, x_rows, step_size, cumul, gram, allowed, d_skip):
    seq_len = d_ssd.shape[0]
    d_ssd_b = d_ssd.astype(jnp.bfloat16)
    x_groups = split_heads(x_rows, HEADDIM)
    grad_b_groups = split_heads(d_ssd_b, HEADDIM)
    grad_groups = split_heads(d_ssd, HEADDIM)
    cum_groups = split_heads(cumul, 1)[..., 0]
    step_groups = split_heads(step_size, 1)[..., 0]
    skip_groups = d_skip.astype(jnp.float32).reshape(HEADS // 4, 4)

    def one_group(carry_gram, group_in):
        x_group, grad_b_group, grad_group, cum_group, step_group, skip_group = group_in
        decays = decay_table(cum_group, allowed)
        step_cols = step_group.T[:, None, :]
        mixing = gram[None] * decays * step_cols
        mixing_b = mixing.astype(jnp.bfloat16)
        grad_float = grad_b_group.astype(jnp.float32)
        d_x = jnp.einsum('hts,thp->shp', mixing_b.astype(jnp.float32), grad_float)
        d_x = d_x + skip_group[None, :, None] * grad_group
        d_mix = jnp.einsum('thp,shp->hts', grad_float, x_group.astype(jnp.float32))
        carry_gram = carry_gram + lax.optimization_barrier(jnp.sum(d_mix * decays * step_cols, axis=0))
        d_kern = d_mix * mixing
        d_cum = (lax.optimization_barrier(jnp.sum(d_kern, axis=2)) - lax.optimization_barrier(jnp.sum(d_kern, axis=1))).T
        d_step = lax.optimization_barrier(jnp.sum(d_mix * gram[None] * decays, axis=1)).T
        return (carry_gram, (d_x, d_cum, d_step))
    d_gram, (dx_groups, dcum_groups, dstep_groups) = lax.scan(one_group, jnp.zeros((seq_len, seq_len), jnp.float32), (x_groups, grad_b_groups, grad_groups, cum_groups, step_groups, skip_groups))
    d_x_rows = join_heads(dx_groups)
    d_cumul = join_heads(dcum_groups[..., None])
    d_step_direct = join_heads(dstep_groups[..., None])
    g_skip = lax.optimization_barrier(jnp.sum((d_ssd * x_rows.astype(jnp.float32)).reshape(seq_len, HEADS, HEADDIM), axis=(0, 2)))
    return (d_x_rows, d_cumul, d_step_direct, d_gram, g_skip)

def layer_backward(d_out, hidden, projected, segment, weights):
    w_in, conv_w, conv_b, dt_bias, a_log, d_skip, gain_one, gain_two, w_out = weights
    inv_rms, normed = input_norm(hidden, gain_one)
    parts_now = mixer_state(projected, segment, weights)
    d_out_b = d_out.astype(jnp.bfloat16)
    g_wout = jnp.dot(parts_now['normed_out'].T, d_out_b, preferred_element_type=jnp.float32)
    d_normed_out = jnp.dot(d_out_b, w_out.T, preferred_element_type=jnp.float32)
    gated_out = parts_now['gated_out']
    inv_two = parts_now['inv_rms_two']
    scaled_two = gain_two.astype(jnp.float32) * d_normed_out
    g_gain_two = lax.optimization_barrier(jnp.sum(d_normed_out * gated_out * inv_two, axis=0))
    d_gated = inv_two * scaled_two - gated_out * inv_two ** 3 * lax.optimization_barrier(jnp.mean(scaled_two * gated_out, axis=-1, keepdims=True))
    d_ssd = d_gated * parts_now['gate_act']
    d_gate = d_gated * parts_now['ssd_out'] * silu_grad(parts_now['gate_in'])
    d_x_rows, d_cumul, d_step_direct, d_gram, g_skip = ssd_backward(d_ssd, parts_now['x_rows'], parts_now['step_size'], parts_now['cumul'], parts_now['gram'], parts_now['allowed'], d_skip)
    rate_vec = parts_now['rate_vec']
    d_rate_sum = jnp.flip(jnp.cumsum(jnp.flip(d_cumul, axis=0), axis=0), axis=0)
    d_step = d_step_direct + d_rate_sum * rate_vec[None, :]
    g_alog = lax.optimization_barrier(jnp.sum(d_rate_sum * parts_now['step_size'], axis=0)) * rate_vec
    d_dt_pre = d_step * jax.nn.sigmoid(parts_now['dt_pre'])
    g_dtbias = lax.optimization_barrier(jnp.sum(d_dt_pre, axis=0))
    d_gram_b = d_gram.astype(jnp.bfloat16)
    d_c_rows = jnp.dot(d_gram_b, parts_now['b_rows'], preferred_element_type=jnp.float32)
    d_b_rows = jnp.dot(d_gram_b.T, parts_now['c_rows'], preferred_element_type=jnp.float32)
    d_act = jnp.concatenate([d_x_rows, d_b_rows, d_c_rows], axis=1)
    conv_in = parts_now['conv_in']
    d_conv_out = d_act * silu_grad(parts_now['conv_out'])
    g_convb = lax.optimization_barrier(jnp.sum(d_conv_out, axis=0))
    tap_sums = []
    d_conv_in = jnp.zeros_like(conv_in)
    for shift_by in range(KCONV):
        masked = d_conv_out * same_doc(segment, shift_by)
        tap_sums.append(lax.optimization_barrier(jnp.sum(masked * shifted(conv_in, shift_by), axis=0)))
        d_conv_in = d_conv_in + pulled(masked * conv_w[shift_by].astype(jnp.float32), shift_by)
    g_convw = jnp.stack(tap_sums)
    d_proj = jnp.concatenate([d_gate, d_conv_in, d_dt_pre], axis=1)
    d_proj_b = d_proj.astype(jnp.bfloat16)
    g_win = jnp.dot(normed.T, d_proj_b, preferred_element_type=jnp.float32)
    d_normed = jnp.dot(d_proj_b, w_in.T, preferred_element_type=jnp.float32)
    scaled_one = gain_one.astype(jnp.float32) * d_normed
    g_gain_one = lax.optimization_barrier(jnp.sum(d_normed * hidden * inv_rms, axis=0))
    d_hidden = d_out + inv_rms * scaled_one - hidden * inv_rms ** 3 * lax.optimization_barrier(jnp.mean(scaled_one * hidden, axis=-1, keepdims=True))
    return (d_hidden, (g_win, g_convw, g_convb, g_dtbias, g_alog, g_skip, g_gain_one, g_gain_two, g_wout))

def adam_update(weights_now, grad_flat, first, second):
    first_new = DECAY_ONE * first + (1.0 - DECAY_ONE) * grad_flat
    second_new = DECAY_TWO * second + (1.0 - DECAY_TWO) * grad_flat * grad_flat
    first_hat = first_new / (1.0 - DECAY_ONE ** STEP)
    second_hat = second_new / (1.0 - DECAY_TWO ** STEP)
    updated = weights_now - LEARN_RATE * (first_hat / (jnp.sqrt(second_hat) + ADAM_EPS) + WEIGHT_DECAY * weights_now)
    return (updated, first_new, second_new)

def reference(inputs, segments, cotangent, params, moment_one, moment_two):
    layer_count = params.shape[0]
    group_count = inputs.shape[0] // SEQ_DEV
    weight_sets = [unpack(params[layer_no].astype(jnp.bfloat16)) for layer_no in range(layer_count)]
    zero_grads = tuple((tuple((jnp.zeros(shape_now, jnp.float32) for shape_now in piece_shapes())) for layer_no in range(layer_count)))

    def per_sequence(totals, seq_in):
        hidden, segment, d_out = seq_in
        stored = []
        for layer_no in range(layer_count):
            projected, hidden_next = layer_forward(hidden, segment, weight_sets[layer_no])
            stored.append((hidden, projected))
            hidden = hidden_next
        new_totals = list(totals)
        for layer_no in reversed(range(layer_count)):
            d_out, grads_now = layer_backward(d_out, stored[layer_no][0], stored[layer_no][1], segment, weight_sets[layer_no])
            new_totals[layer_no] = jax.tree.map(jnp.add, totals[layer_no], grads_now)
        return (tuple(new_totals), (hidden, d_out))

    def per_group(totals, group_in):
        partial_sums, outs_now = lax.scan(per_sequence, zero_grads, group_in)
        rounded = lax.optimization_barrier(jax.tree.map(lambda value: value.astype(jnp.bfloat16), partial_sums))
        added = jax.tree.map(lambda total, value: total + value.astype(jnp.float32), totals, rounded)
        return (added, outs_now)
    grouped = (inputs.reshape((group_count, SEQ_DEV) + inputs.shape[1:]), segments.reshape((group_count, SEQ_DEV) + segments.shape[1:]), cotangent.reshape((group_count, SEQ_DEV) + cotangent.shape[1:]))
    totals, (outputs, d_inputs) = lax.scan(per_group, zero_grads, grouped)
    outputs = outputs.reshape(inputs.shape)
    d_inputs = d_inputs.reshape(inputs.shape)
    grad_flat = jnp.stack([pack(totals[layer_no], PFLAT) for layer_no in range(layer_count)])
    new_params, new_one, new_two = adam_update(params, grad_flat, moment_one, moment_two)
    return (outputs, d_inputs, grad_flat, new_params, new_one, new_two)
```

```python
import functools
import math

import jax
import jax.numpy as jnp
from jax import lax
from jax.experimental import pallas as pl
from jax.experimental.pallas import tpu as pltpu
from jax.sharding import PartitionSpec as P

D = 1536
DI = 3072
HEADS = 48
STATE = 128
HEADDIM = 64
KCONV = 4
STEP = 4
DCONV = 3328
DPROJ = 6448
T = 512
XW = 3456
GH = 8
NG = HEADS // GH
GW = GH * HEADDIM
BLK = 128
NB = T // BLK

NORM_EPS = 1e-05
ADAM_EPS = 1e-08
LEARN_RATE = 0.003
DECAY_ONE = 0.9
DECAY_TWO = 0.95
WEIGHT_DECAY = 0.1
LOG2E = math.log2(math.e)
LN2 = math.log(2.0)

ALL = ("dp", "fsdp")
BF = jnp.bfloat16
F32 = jnp.float32

SMALLS = [KCONV * DCONV, DCONV, HEADS, HEADS, HEADS, D, DI]
SMALL_AT = D * DPROJ
SMALL_N = sum(SMALLS)
SMALL_PAD = -(-SMALL_N // 1024) * 1024
WOUT_AT = SMALL_AT + SMALL_N


def dot(a, b, ca=1, cb=0):
    return lax.dot_general(a, b, (((ca,), (cb,)), ((), ())), preferred_element_type=F32)


class Rows:
    def __init__(self, n, shard, base, width, total):
        self.n, self.shard, self.width = n, shard, width
        self.per = total // n
        self.span = (shard + width - 2) // width + 1
        self.first = [(shard * d - base) // width for d in range(n)]
        self.col = [(shard * d - base) % width for d in range(n)]
        edges = []
        for s in range(n):
            last = (shard * (s + 1) - base - 1) // width
            low, high = max(self.first[s], 0), min(last + 1, total)
            if low < high:
                edges += [(s, t) for t in range(low // self.per, (high - 1) // self.per + 1)]
        degree = max(
            max(sum(e[k] == d for e in edges) for d in range(n)) for k in range(2)
        )
        self.rounds = [edges[k::degree] for k in range(degree)]
        self.total = total

    def pick(self, table, me):
        return jnp.asarray(table, jnp.int32)[me]

    def to_blocks(self, flat, me):
        wide = jnp.zeros((self.span * self.width,), flat.dtype)
        wide = lax.dynamic_update_slice(wide, flat, (self.pick(self.col, me),))
        rows = wide.reshape(self.span, self.width)
        at = self.pick(self.first, me) + jnp.arange(self.span)
        rows = jnp.where(((at >= 0) & (at < self.total))[:, None], rows, 0)
        rows = jnp.pad(rows, ((self.per, self.per), (0, 0)))
        out = []
        for edges in self.rounds:
            table = [0] * self.n
            for s, t in edges:
                table[s] = self.per * t - self.first[s] + self.per
            out.append(lax.dynamic_slice(rows, (self.pick(table, me), 0), (self.per, self.width)))
        return out

    def send(self, messages):
        parts = [lax.ppermute(m, ALL, e) for m, e in zip(messages, self.rounds)]
        return functools.reduce(jnp.add, parts)

    def to_flat(self, block, me):
        rows = jnp.zeros((self.span + 2 * self.per, self.width), F32)
        for edges in self.rounds:
            got = lax.ppermute(block, ALL, [(t, s) for s, t in edges]).astype(F32)
            table = [0] * self.n
            for s, t in edges:
                table[s] = self.per * t - self.first[s] + self.per
            rows = lax.dynamic_update_slice(rows, got, (self.pick(table, me), 0))
        rows = rows[self.per : self.per + self.span]
        return lax.dynamic_slice(rows.reshape(-1), (self.pick(self.col, me),), (self.shard,))


def sum_all(v, n):
    k = 1
    while k < n:
        v = v + lax.ppermute(v, ALL, [(i, i ^ k) for i in range(n)])
        k *= 2
    return v


def params(steps=1):
    return pltpu.CompilerParams(
        dimension_semantics=("arbitrary",) * steps, vmem_limit_bytes=56 * 1024 * 1024
    )


def full(shape):
    return pl.BlockSpec(shape, lambda *_: (0,) * len(shape))


def dt_kernel(p_ref, bias_ref, alog_ref, dt_ref, step_ref, cum_ref, cs_ref, cumt_ref, cst_ref):
    dt = p_ref[...] + bias_ref[...]
    step = jnp.maximum(dt, 0.0) + jnp.log1p(jnp.exp(-jnp.abs(dt)))
    acc = step * -jnp.exp(alog_ref[...]) * LOG2E
    row = lax.broadcasted_iota(jnp.int32, acc.shape, 0)
    k = 1
    while k < T:
        acc = acc + jnp.where(row >= k, pltpu.roll(acc, k, 0), 0.0)
        k *= 2
    cs = acc - jnp.log(step) * LOG2E
    dt_ref[...] = dt
    step_ref[...] = step
    cum_ref[...] = acc
    cs_ref[...] = cs
    cumt_ref[...] = acc.T
    cst_ref[...] = cs.T


def dt_call(projx, bias, alog):
    col = jax.ShapeDtypeStruct((T, 128), F32)
    row = jax.ShapeDtypeStruct((128, T), F32)
    return pl.pallas_call(
        dt_kernel,
        grid=(1,),
        in_specs=[
            pl.BlockSpec((T, 128), lambda i: (0, DCONV // 128)),
            full((1, 128)),
            full((1, 128)),
        ],
        out_specs=[full((T, 128))] * 4 + [full((128, T))] * 2,
        out_shape=[col] * 4 + [row] * 2,
        compiler_params=params(),
        name="dt_fwd",
    )(projx, bias, alog)


def conv_taps(ci, w_ref, m_ref):
    acc = w_ref[KCONV : KCONV + 1, :] + w_ref[0:1, :] * ci
    taps = [ci]
    for k in range(1, KCONV):
        tap = pltpu.roll(ci, k, 0) * m_ref[:, k : k + 1]
        acc = acc + w_ref[k : k + 1, :] * tap
        taps.append(tap)
    return acc, taps


def conv_fwd_kernel(p_ref, w_ref, m_ref, o_ref):
    acc, _ = conv_taps(p_ref[...], w_ref, m_ref)
    o_ref[...] = (acc * jax.nn.sigmoid(acc)).astype(BF)


def conv_fwd(projx, wrow, masks):
    cw = 256
    return pl.pallas_call(
        conv_fwd_kernel,
        grid=(DCONV // cw,),
        in_specs=[
            pl.BlockSpec((T, cw), lambda i: (0, i)),
            pl.BlockSpec((8, cw), lambda i: (0, i)),
            full((T, 8)),
        ],
        out_specs=pl.BlockSpec((T, cw), lambda i: (0, i)),
        out_shape=jax.ShapeDtypeStruct((T, DCONV), BF),
        compiler_params=params(),
        name="conv_fwd",
    )(projx, wrow, masks)


def ssd_fwd_kernel(x_ref, b_ref, c_ref, sc_ref, sr_ref, cum_ref, cst_ref, y_ref, g_ref):
    @pl.when(pl.program_id(0) == 0)
    def _():
        gram = dot(c_ref[...], b_ref[...], 1, 1)
        t = lax.broadcasted_iota(jnp.int32, (T, T), 0)
        s = lax.broadcasted_iota(jnp.int32, (T, T), 1)
        g_ref[...] = jnp.where((t >= s) & (sc_ref[...] == sr_ref[...]), gram, 0.0)

    causal = lax.broadcasted_iota(jnp.int32, (BLK, BLK), 0) >= lax.broadcasted_iota(
        jnp.int32, (BLK, BLK), 1
    )
    for h in range(GH):
        lanes = slice(h * HEADDIM, (h + 1) * HEADDIM)
        for i in range(NB):
            lo, hi = i * BLK, (i + 1) * BLK
            cum = cum_ref[0, lo:hi, h : h + 1]
            diag = jnp.where(causal, cum - cst_ref[h : h + 1, lo:hi], -1e30)
            mix = (g_ref[lo:hi, lo:hi] * jnp.exp2(diag)).astype(BF)
            y = dot(mix, x_ref[lo:hi, lanes])
            if i:
                off = jnp.exp2(cum - cst_ref[h : h + 1, :lo])
                mix = (g_ref[lo:hi, :lo] * off).astype(BF)
                y = y + dot(mix, x_ref[:lo, lanes])
            y_ref[lo:hi, lanes] = y


def ssd_fwd(act, segc, segr, cumg, cst):
    return pl.pallas_call(
        ssd_fwd_kernel,
        grid=(NG,),
        in_specs=[
            pl.BlockSpec((T, GW), lambda i: (0, i)),
            pl.BlockSpec((T, STATE), lambda i: (0, DI // STATE)),
            pl.BlockSpec((T, STATE), lambda i: (0, DI // STATE + 1)),
            full((T, 1)),
            full((1, T)),
            pl.BlockSpec((1, T, GH), lambda i: (i, 0, 0)),
            pl.BlockSpec((GH, T), lambda i: (i, 0)),
        ],
        out_specs=pl.BlockSpec((T, GW), lambda i: (0, i)),
        out_shape=jax.ShapeDtypeStruct((T, DI), F32),
        scratch_shapes=[pltpu.VMEM((T, T), F32)],
        compiler_params=params(),
        name="ssd_fwd",
    )(act, act, act, segc, segr, cumg, cst)


def ssd_bwd_kernel(
    x_ref, dy_ref, y_ref, b_ref, c_ref, sc_ref, sr_ref, csg_ref, cumt_ref,
    dx_ref, dcum_ref, col_ref, dbc_ref, g_ref, dg_ref,
):
    step = pl.program_id(0)

    @pl.when(step == 0)
    def _():
        gram = dot(b_ref[...], c_ref[...], 1, 1)
        s = lax.broadcasted_iota(jnp.int32, (T, T), 0)
        t = lax.broadcasted_iota(jnp.int32, (T, T), 1)
        g_ref[...] = jnp.where((t >= s) & (sc_ref[...] == sr_ref[...]), gram, 0.0)
        dg_ref[...] = jnp.zeros_like(dg_ref)

    causal = lax.broadcasted_iota(jnp.int32, (BLK, BLK), 1) >= lax.broadcasted_iota(
        jnp.int32, (BLK, BLK), 0
    )
    for h in range(GH):
        lanes = slice(h * HEADDIM, (h + 1) * HEADDIM)
        for i in range(NB):
            lo, hi = i * BLK, (i + 1) * BLK
            cs = csg_ref[0, lo:hi, h : h + 1]
            xb = x_ref[lo:hi, lanes]
            diag = jnp.exp2(jnp.where(causal, cumt_ref[h : h + 1, lo:hi] - cs, -1e30))
            mix = (g_ref[lo:hi, lo:hi] * diag).astype(BF)
            dx = dot(mix, dy_ref[lo:hi, lanes])
            dg_ref[lo:hi, lo:hi] += dot(xb, dy_ref[lo:hi, lanes], 1, 1) * diag
            if hi < T:
                off = jnp.exp2(cumt_ref[h : h + 1, hi:] - cs)
                mix = (g_ref[lo:hi, hi:] * off).astype(BF)
                dx = dx + dot(mix, dy_ref[hi:, lanes])
                dg_ref[lo:hi, hi:] += dot(xb, dy_ref[hi:, lanes], 1, 1) * off
            dx_ref[lo:hi, lanes] = dx
            col = jnp.sum(xb.astype(F32) * dx, axis=1, keepdims=True)
            row = jnp.sum(dy_ref[lo:hi, lanes].astype(F32) * y_ref[lo:hi, lanes], axis=1, keepdims=True)
            col_ref[0, lo:hi, h : h + 1] = col
            dcum_ref[0, lo:hi, h : h + 1] = row - col

    @pl.when(step == NG - 1)
    def _():
        s = lax.broadcasted_iota(jnp.int32, (T, T), 0)
        t = lax.broadcasted_iota(jnp.int32, (T, T), 1)
        dg = jnp.where((t >= s) & (sc_ref[...] == sr_ref[...]), dg_ref[...], 0.0)
        dbc_ref[:, :STATE] = dot(dg.astype(BF), c_ref[...])
        dbc_ref[:, STATE:] = dot(dg.T.astype(BF), b_ref[...])


def ssd_bwd(act, dy, y, segc, segr, csg, cumt):
    wide = pl.BlockSpec((T, GW), lambda i: (0, i))
    group = pl.BlockSpec((1, T, GH), lambda i: (i, 0, 0))
    return pl.pallas_call(
        ssd_bwd_kernel,
        grid=(NG,),
        in_specs=[
            wide,
            wide,
            wide,
            pl.BlockSpec((T, STATE), lambda i: (0, DI // STATE)),
            pl.BlockSpec((T, STATE), lambda i: (0, DI // STATE + 1)),
            full((T, 1)),
            full((1, T)),
            group,
            pl.BlockSpec((GH, T), lambda i: (i, 0)),
        ],
        out_specs=[wide, group, group, full((T, 2 * STATE))],
        out_shape=[
            jax.ShapeDtypeStruct((T, DI), F32),
            jax.ShapeDtypeStruct((NG, T, GH), F32),
            jax.ShapeDtypeStruct((NG, T, GH), F32),
            jax.ShapeDtypeStruct((T, 2 * STATE), F32),
        ],
        scratch_shapes=[pltpu.VMEM((T, T), F32), pltpu.VMEM((T, T), F32)],
        compiler_params=params(),
        name="ssd_bwd",
    )(act, dy, y, act, act, segc, segr, csg, cumt)


def gate_fwd_kernel(y_ref, x_ref, g_ref, row_ref, o_ref):
    gate = g_ref[...]
    ssd = y_ref[...] + row_ref[0:1, :] * x_ref[...].astype(F32)
    gated = ssd * (gate * jax.nn.sigmoid(gate))
    inv = lax.rsqrt(jnp.mean(gated * gated, axis=1, keepdims=True) + NORM_EPS)
    o_ref[...] = (gated * inv * row_ref[1:2, :]).astype(BF)


def gate_fwd(y, act, gate, rows):
    rb = 128
    wide = pl.BlockSpec((rb, DI), lambda i: (i, 0))
    return pl.pallas_call(
        gate_fwd_kernel,
        grid=(T // rb,),
        in_specs=[wide, wide, wide, full((8, DI))],
        out_specs=wide,
        out_shape=jax.ShapeDtypeStruct((T, DI), BF),
        compiler_params=params(),
        name="gate_fwd",
    )(y, act, gate, rows)


def gate_bwd_kernel(y_ref, x_ref, g_ref, dn_ref, row_ref, dy_ref, dg_ref, sum_ref):
    gate = g_ref[...]
    dn = dn_ref[...]
    x = x_ref[...].astype(F32)
    sig = jax.nn.sigmoid(gate)
    act = gate * sig
    ssd = y_ref[...] + row_ref[0:1, :] * x
    gated = ssd * act
    inv = lax.rsqrt(jnp.mean(gated * gated, axis=1, keepdims=True) + NORM_EPS)
    e = row_ref[1:2, :] * dn
    mean = jnp.mean(e * gated, axis=1, keepdims=True)
    d_gated = inv * e - gated * (inv * inv * inv * mean)
    d_ssd = d_gated * act
    dy_ref[...] = d_ssd.astype(BF)
    dg_ref[...] = (d_gated * ssd * (sig * (1.0 + gate * (1.0 - sig)))).astype(BF)

    @pl.when(pl.program_id(0) == 0)
    def _():
        sum_ref[...] = jnp.zeros_like(sum_ref)

    sum_ref[0:1, :] += jnp.sum(dn * gated * inv, axis=0, keepdims=True)
    sum_ref[1:2, :] += jnp.sum(d_ssd * x, axis=0, keepdims=True)


def gate_bwd(y, act, gate, dn, rows):
    rb = 64
    wide = pl.BlockSpec((rb, DI), lambda i: (i, 0))
    return pl.pallas_call(
        gate_bwd_kernel,
        grid=(T // rb,),
        in_specs=[wide, wide, wide, wide, full((8, DI))],
        out_specs=[wide, wide, full((8, DI))],
        out_shape=[
            jax.ShapeDtypeStruct((T, DI), BF),
            jax.ShapeDtypeStruct((T, DI), BF),
            jax.ShapeDtypeStruct((8, DI), F32),
        ],
        compiler_params=params(),
        name="gate_bwd",
    )(y, act, gate, dn, rows)


def conv_bwd_kernel(p_ref, dx_ref, dy_ref, dbc_ref, w_ref, skip_ref, m_ref, o_ref, s_ref):
    acc, taps = conv_taps(p_ref[...], w_ref, m_ref)
    sig = jax.nn.sigmoid(acc)
    last = pl.program_id(0) == pl.num_programs(0) - 1
    d_act = jnp.where(last, dbc_ref[...], dx_ref[...] + skip_ref[...] * dy_ref[...].astype(F32))
    d_out = d_act * (sig * (1.0 + acc * (1.0 - sig)))
    d_in = d_out * w_ref[0:1, :]
    s_ref[0:1, :] = jnp.sum(d_out * taps[0], axis=0, keepdims=True)
    for k in range(1, KCONV):
        s_ref[k : k + 1, :] = jnp.sum(d_out * taps[k], axis=0, keepdims=True)
        d_in = d_in + pltpu.roll(d_out * m_ref[:, k : k + 1], T - k, 0) * w_ref[k : k + 1, :]
    s_ref[KCONV : KCONV + 1, :] = jnp.sum(d_out, axis=0, keepdims=True)
    s_ref[KCONV + 1 :, :] = jnp.zeros_like(s_ref[KCONV + 1 :, :])
    o_ref[...] = d_in.astype(BF)


def conv_bwd(projx, dx, dy, dbc, wrow, skip, masks):
    cw = 256
    top = DI // cw - 1
    clip = pl.BlockSpec((T, cw), lambda i: (0, jnp.minimum(i, top)))
    return pl.pallas_call(
        conv_bwd_kernel,
        grid=(DCONV // cw,),
        in_specs=[
            pl.BlockSpec((T, cw), lambda i: (0, i)),
            clip,
            clip,
            full((T, cw)),
            pl.BlockSpec((8, cw), lambda i: (0, i)),
            pl.BlockSpec((1, cw), lambda i: (0, jnp.minimum(i, top))),
            full((T, 8)),
        ],
        out_specs=[pl.BlockSpec((T, cw), lambda i: (0, i)), pl.BlockSpec((8, cw), lambda i: (0, i))],
        out_shape=[
            jax.ShapeDtypeStruct((T, DCONV), BF),
            jax.ShapeDtypeStruct((8, DCONV), F32),
        ],
        compiler_params=params(),
        name="conv_bwd",
    )(projx, dx, dy, dbc, wrow, skip, masks)


def dt_bwd_kernel(dcum_ref, col_ref, dt_ref, step_ref, alog_ref, o_ref, s_ref):
    acc = dcum_ref[...]
    row = lax.broadcasted_iota(jnp.int32, acc.shape, 0)
    k = 1
    while k < T:
        acc = acc + jnp.where(row < T - k, pltpu.roll(acc, T - k, 0), 0.0)
        k *= 2
    rate = -jnp.exp(alog_ref[...])
    step = step_ref[...]
    sig = jax.nn.sigmoid(dt_ref[...])
    ratio = jnp.where(step > 0.0, sig / jnp.where(step > 0.0, step, 1.0), 1.0)
    d_dt = col_ref[...] * ratio + acc * rate * sig
    lane = lax.broadcasted_iota(jnp.int32, acc.shape, 1)
    d_dt = jnp.where(lane < HEADS, d_dt, 0.0)
    o_ref[...] = d_dt.astype(BF)
    s_ref[0:1, :] = jnp.sum(d_dt, axis=0, keepdims=True)
    s_ref[1:2, :] = rate * jnp.sum(acc * step, axis=0, keepdims=True)
    s_ref[2:, :] = jnp.zeros_like(s_ref[2:, :])


def dt_bwd(dcum, col, dt, step, alog):
    return pl.pallas_call(
        dt_bwd_kernel,
        grid=(1,),
        in_specs=[full((T, 128))] * 4 + [full((1, 128))],
        out_specs=[full((T, 128)), full((8, 128))],
        out_shape=[jax.ShapeDtypeStruct((T, 128), BF), jax.ShapeDtypeStruct((8, 128), F32)],
        compiler_params=params(),
        name="dt_bwd",
    )(dcum, col, dt, step, alog)


def grouped(v):
    return v[:, :HEADS].reshape(T, NG, GH).transpose(1, 0, 2)


def ungrouped(v):
    return jnp.pad(v.transpose(1, 0, 2).reshape(T, HEADS), ((0, 0), (0, 128 - HEADS)))


def lanes128(v):
    return jnp.pad(v, (0, 128 - v.shape[0]))[None, :]


def adam(weights, grads, first, second):
    first_new = DECAY_ONE * first + (1.0 - DECAY_ONE) * grads
    second_new = DECAY_TWO * second + (1.0 - DECAY_TWO) * grads * grads
    first_hat = first_new / (1.0 - DECAY_ONE**STEP)
    second_hat = second_new / (1.0 - DECAY_TWO**STEP)
    updated = weights - LEARN_RATE * (
        first_hat / (jnp.sqrt(second_hat) + ADAM_EPS) + WEIGHT_DECAY * weights
    )
    return updated, first_new, second_new


def gather(block):
    return lax.all_gather(block, ALL, axis=0, tiled=True)


def scatter(whole):
    return lax.optimization_barrier(lax.psum_scatter(whole, ALL, scatter_dimension=0, tiled=True))


def local(n, inputs, segments, cotangent, params, moment_one, moment_two):
    shard = params.shape[1]
    me = lax.axis_index(ALL)
    rows_in = Rows(n, shard, 0, DPROJ, D)
    rows_out = Rows(n, shard, WOUT_AT, D, DI)
    flat = params[0].astype(BF)

    msgs = rows_in.to_blocks(flat, me)
    block_x = rows_in.send([m[:, DI:] for m in msgs])
    block_x = jnp.pad(block_x, ((0, 0), (0, XW - block_x.shape[1])))
    block_g = rows_in.send([m[:, :DI] for m in msgs])
    block_o = rows_out.send(rows_out.to_blocks(flat, me))

    near = jnp.pad(flat, (SMALL_PAD, SMALL_PAD))
    at = jnp.clip(SMALL_AT - me * shard + SMALL_PAD, 0, shard + SMALL_PAD)
    smalls = lax.dynamic_slice(near, (at,), (SMALL_PAD,)).reshape(-1, 128)
    smalls = sum_all(smalls, n).reshape(-1).astype(F32)
    pieces = []
    at = 0
    for count in SMALLS:
        pieces.append(smalls[at : at + count])
        at += count
    conv_w, conv_b, dt_bias, a_log, d_skip, gain_one, gain_two = pieces
    wrow = jnp.concatenate(
        [conv_w.reshape(KCONV, DCONV), conv_b[None], jnp.zeros((3, DCONV), F32)], axis=0
    )
    skip_row = jnp.repeat(d_skip, HEADDIM)[None, :]
    gate_rows = jnp.concatenate([skip_row, gain_two[None], jnp.zeros((6, DI), F32)], axis=0)
    bias_row, alog_row = lanes128(dt_bias), lanes128(a_log)

    w_x = gather(block_x)
    w_g = gather(block_g)
    w_o = gather(block_o)

    hidden, d_out, seg = inputs[0], cotangent[0], segments[0]
    inv_rms = lax.rsqrt(jnp.mean(hidden * hidden, axis=-1, keepdims=True) + NORM_EPS)
    normed = (hidden * inv_rms * gain_one[None, :]).astype(BF)
    segc, segr = seg[:, None], seg[None, :]
    index = jnp.arange(T, dtype=jnp.int32)
    masks = jnp.stack(
        [(index >= k) & (jnp.roll(seg, k) == seg) for k in range(KCONV)] + [index < 0] * 4, axis=1
    ).astype(F32)

    projx = dot(normed, w_x)
    dt, step, cum, cs, cumt, cst = dt_call(projx, bias_row, alog_row)
    act = conv_fwd(projx, wrow, masks)
    y = ssd_fwd(act, segc, segr, grouped(cum), cst)
    gate = dot(normed, w_g)
    normed_out = gate_fwd(y, act, gate, gate_rows)
    d_out_b = d_out.astype(BF)
    g_out = dot(normed_out, d_out_b, 0, 0).astype(BF)
    s_out = scatter(g_out)

    output = hidden + dot(normed_out, w_o)
    d_no = dot(d_out_b, w_o, 1, 1)
    dy, d_gate, gate_sums = gate_bwd(y, act, gate, d_no, gate_rows)
    g_gate = dot(normed, d_gate, 0, 0).astype(BF)
    s_gate = scatter(g_gate)
    dx, dcum, col, dbc = ssd_bwd(act, dy, y, segc, segr, grouped(cs), cumt)
    d_dt, dt_sums = dt_bwd(ungrouped(dcum), ungrouped(col), dt, step, alog_row)
    d_ci, conv_sums = conv_bwd(projx, dx, dy, dbc, wrow, skip_row, masks)
    d_xp = jnp.concatenate([d_ci, d_dt], axis=1)
    g_x = dot(normed, d_xp, 0, 0).astype(BF)
    s_x = scatter(g_x)

    d_normed = dot(d_gate, w_g, 1, 1) + dot(d_xp, w_x, 1, 1)
    e1 = gain_one[None, :] * d_normed
    g_gain_one = jnp.sum(d_normed * hidden * inv_rms, axis=0)
    d_hidden = (
        d_out + inv_rms * e1 - hidden * inv_rms**3 * jnp.mean(e1 * hidden, axis=-1, keepdims=True)
    )
    g_skip = jnp.sum(gate_sums[1].reshape(HEADS, HEADDIM), axis=1)
    g_small = jnp.concatenate(
        [
            conv_sums[: KCONV + 1].reshape(-1),
            dt_sums[0, :HEADS],
            dt_sums[1, :HEADS],
            g_skip,
            g_gain_one,
            gate_sums[0],
            jnp.zeros((SMALL_PAD - SMALL_N,), F32),
        ]
    )
    g_small = sum_all(g_small.reshape(-1, 128), n).reshape(-1)

    s_in = jnp.concatenate([s_gate, s_x[:, : DPROJ - DI]], axis=1)
    grads = rows_in.to_flat(s_in, me) + rows_out.to_flat(s_out, me)
    near = jnp.pad(g_small, (shard, shard))
    at = jnp.clip(me * shard - SMALL_AT + shard, 0, SMALL_PAD + shard)
    grads = (grads + lax.dynamic_slice(near, (at,), (shard,)))[None]
    new_params, new_one, new_two = adam(params, grads, moment_one, moment_two)
    return (output[None], d_hidden[None], grads, new_params, new_one, new_two)


def solution(mesh):
    n = mesh.size
    seq = P(ALL, None, None)
    flat = P(None, ALL)
    return jax.shard_map(
        functools.partial(local, n),
        mesh=mesh,
        in_specs=(seq, P(ALL, None), seq, flat, flat, flat),
        out_specs=(seq, seq, flat, flat, flat, flat),
        check_vma=False,
    )
```
